32 devices in a mesh: row: 8 (over y, x, core), col: 4 (over z).
Axes of the slice: x: 2, y: 2, z: 4, core: 2. Of those that a mesh axis runs over, the one named last changes fastest.
Arguments:
- a_panels: bfloat16 [16384, 1024], P('row', 'col'), may hold values from -6 to 6
- a_mask: int32 [128, 8], P('row', 'col'), may hold values 0 or 1
- b_panels: bfloat16 [1024, 4096], P('row', 'col'), may hold values from -0.1875 to 0.1875
- b_mask: int32 [8, 32], P('row', 'col'), may hold values 0 or 1
- owner_map: int32 [128, 1], P('row'), may hold values from 0 to 7; in each aligned block of 16 rows (0 to 15, 16 to 31, ...) at most 2 rows name the same one
Outputs:
- owned: bfloat16 [16384, 4096], P('row', 'col')
The draws below stay inside these ranges and needn't reach their ends.
Inputs may be any that keep to these rules, and one draw needn't show every extreme that they name: `owner_map`: within each aligned block of 16 tile rows (the tile rows of one grid row) no owner is named more than 2 times, a bound that some block reaches.
All inputs are finite; a program needn't handle non-finite values. No bound on the sum of `a_mask` or of `b_mask` on one device may be relied on, other than what follows from the above.
Results may differ from the reference program's by a relative error of at most 0.001.
Values may be sent and summed in bfloat16 or wider, within the bound.
No kernel may reach another device: no remote copies, remote signals or barrier semaphores. Data moves between devices by JAX's collectives and lax.ppermute only.
A program may use at most 128 MiB of HBM per device.

```python
import math
import jax
import jax.numpy as jnp
import numpy as np
from jax import lax

TILE = 128
MT = 16
SLOTS = 2
PANELS = 8
M_ROWS = 16384
K_INNER = 1024
N_COLS = 4096
N_ROW = 8


def plant(array, rng, smallest, largest):
    longest = array.shape.index(max(array.shape))
    spots = []
    for shift in (0, 1):
        where = [jax.random.randint(jax.random.fold_in(rng, axis), (), 0, length) for axis, length in enumerate(array.shape)]
        where[longest] = (where[longest] + shift) % array.shape[longest]
        spots.append(tuple(where))
    return array.at[spots[0]].set(smallest).at[spots[1]].set(largest)


def level_of(key, dims, shards, smallest, top_value):
    level = 1.0
    for axis_at, blocks in shards:
        heights = jax.random.uniform(jax.random.fold_in(jax.random.fold_in(key, 6), axis_at), (blocks,), jnp.float32, smallest / len(shards), top_value / len(shards))
        level = level * jnp.repeat(jnp.exp(heights), dims[axis_at] // blocks).reshape((-1,) + (1,) * (len(dims) - 1 - axis_at))
    return level


def deal_out(own_key, own, number, rows, number_of, top, reach, skew):
    ranking = jax.random.permutation(own_key, number_of)
    crowded, ordinary = portions_of(number_of, rows * top, reach, skew, True), portions_of(number_of, rows * top, reach, skew, False)
    places = jnp.arange(number_of)

    def named(sizes, turn):
        used = int((sizes > 0).sum())
        fixed = max(1, used // 4)
        shifted = fixed + (places - fixed + turn * (used - fixed)) % max(1, number_of - fixed)
        return jnp.zeros((number_of,), jnp.int32).at[ranking[jnp.where(places < fixed, places, shifted)]].set(jnp.asarray(sizes, jnp.int32))

    sizes = jnp.where(number % 4 == 0, named(crowded, number // 4), named(ordinary, number - number // 4 - 1))
    mixed = jax.random.permutation(jax.random.fold_in(own, 3), number_of)
    donor, taker = mixed[0:number_of // 2 * 2:2], mixed[1:number_of // 2 * 2:2]
    margin = jnp.minimum(sizes[donor] - 1, reach - sizes[taker]) // 2
    margin = jnp.where((donor == ranking[0]) | (taker == ranking[0]) | (sizes[taker] == 0), 0, jnp.maximum(margin, 0))
    shifted = jax.random.randint(jax.random.fold_in(own, 4), (number_of // 2,), 0, 1 << 20) % (margin + 1)
    sizes = sizes.at[donor].add(-shifted).at[taker].add(shifted)
    labels = jnp.searchsorted(jnp.cumsum(sizes), jnp.arange(rows * top), side="right").astype(jnp.int32)
    listing = labels.reshape(top, rows).T
    listing = listing[jax.random.permutation(jax.random.fold_in(own, 1), rows)]
    turn = jax.random.randint(jax.random.fold_in(own, 2), (rows, 1), 0, top)
    return jnp.take_along_axis(listing, (jnp.arange(top)[None, :] + turn) % top, axis=1)


def portions_of(number_of, total, most, slope, full):
    loads = [(1 << 20) // math.isqrt(grade ** slope) + 1 for grade in range(1, number_of + 1)]
    largest = most if full else min(most, max(-(-total // number_of), total * loads[0] // sum(loads)))
    least = 1 if total - largest >= number_of - 1 else 0
    holding, surplus = [largest] + [least] * (number_of - 1), total - largest - least * (number_of - 1)
    while surplus > 0:
        candidates = [i for i in range(1, number_of) if holding[i] < largest] or [i for i in range(1, number_of) if holding[i] < most]
        whole, budget = sum([loads[i] for i in candidates]), surplus
        for i in candidates:
            more = min(most - holding[i], max(1, budget * loads[i] // whole), surplus)
            holding[i] = holding[i] + more
            surplus = surplus - more
    return np.array(holding)


def bell_draw(stream_key, shape, width, most, pieces=(), held_as=jnp.bfloat16):
    values = jax.random.normal(stream_key, shape, jnp.float32) * width
    if len(pieces) > 0:
        values = level_of(stream_key, shape, pieces, -0.22, 0.18) * values
    return jnp.clip(values, min=-most, max=most).astype(held_as)


def setup_inputs(seed: int = 0) -> dict:
    key_of = jax.random.split(jax.random.key(seed), 6)
    a_panels = bell_draw(key_of[0], (M_ROWS, K_INNER), 1.0, 6.0, ((0, 8), (1, 4)))
    a_mask = plant((jax.random.randint(key_of[1], (M_ROWS // TILE, PANELS), 0, 3) < 2).astype(jnp.int32), jax.random.fold_in(key_of[1], 1), 0, 1)
    b_panels = bell_draw(key_of[2], (K_INNER, N_COLS), K_INNER ** -0.5, 0.1875, ((0, 8), (1, 4)))
    b_mask = plant((jax.random.randint(key_of[3], (PANELS, N_COLS // TILE), 0, 3) < 2).astype(jnp.int32), jax.random.fold_in(key_of[3], 1), 0, 1)
    owner_map_keys = jax.random.split(jax.random.fold_in(key_of[4], 1), (MT * PANELS) // MT)
    owner_map_turns = jax.random.permutation(jax.random.fold_in(key_of[4], 3), (MT * PANELS) // MT)
    owner_map = jax.vmap(lambda own, number: deal_out(jax.random.fold_in(key_of[4], 2), own, number, MT, PANELS, 1, SLOTS, 2))(owner_map_keys, owner_map_turns).reshape((MT * PANELS, 1))
    return {"a_panels": a_panels, "a_mask": a_mask, "b_panels": b_panels, "b_mask": b_mask, "owner_map": owner_map}


def expand_mask(mask):
    wide = jnp.repeat(mask.astype(jnp.bfloat16), TILE, axis=0)
    return jnp.repeat(wide, TILE, axis=1)


def pack_rows(product, owners):
    tile_rows = owners.shape[0]
    same = owners[:, None] == owners[None, :]
    earlier = jnp.arange(tile_rows, dtype=jnp.int32)[None, :] < jnp.arange(tile_rows, dtype=jnp.int32)[:, None]
    rank = jnp.sum(jnp.where(same & earlier, 1, 0).astype(jnp.int32), axis=1).astype(jnp.int32)
    slot_id = owners * SLOTS + rank
    select = (jnp.arange(N_ROW * SLOTS, dtype=jnp.int32)[:, None] == slot_id[None, :]).astype(jnp.bfloat16)
    flat = product.reshape(tile_rows, -1)
    packed = jnp.dot(select, flat, preferred_element_type=jnp.float32).astype(jnp.bfloat16)
    return packed.reshape(N_ROW, SLOTS * TILE, -1)


def reference(a_panels, a_mask, b_panels, b_mask, owner_map):
    b_eff = b_panels * expand_mask(b_mask)
    a_blocks = a_panels.reshape(N_ROW, MT * TILE, -1)
    m_blocks = a_mask.reshape(N_ROW, MT, -1)
    o_blocks = owner_map.reshape(N_ROW, MT)

    def one_block(items):
        block_a, block_m, block_o = items
        a_eff = block_a * expand_mask(block_m)
        product = jnp.dot(a_eff, b_eff, preferred_element_type=jnp.float32).astype(jnp.bfloat16)
        return pack_rows(product, block_o)

    packed = lax.map(one_block, (a_blocks, m_blocks, o_blocks))
    owned = jnp.transpose(packed, (1, 0, 2, 3))
    return owned.reshape(-1, packed.shape[-1])
```

```python
import functools
import jax
import jax.numpy as jnp
from jax import lax
from jax.experimental import pallas as pl
from jax.experimental.pallas import tpu as pltpu
from jax.sharding import PartitionSpec as P

SLOTS = 2
SMEM_SPEC = pl.BlockSpec(memory_space=pltpu.SMEM)


def pack_kernel(grid_rows, by_distance, owner_ref, am_ref, bm_ref, a_ref, b_ref, *rest):
    outs, b_out, inv, used = rest[:grid_rows], rest[grid_rows], rest[-2], rest[-1]
    tile_rows, inner = am_ref.shape
    tile = a_ref.shape[0] // tile_rows
    wide = a_ref.shape[1] // inner
    me = lax.axis_index("row")

    def clear(i, carry):
        inv[i] = -1
        return carry

    def clear_used(i, carry):
        used[i] = 0
        return carry

    def place(t, carry):
        owner = owner_ref[t, 0]
        slot = used[owner]
        inv[owner * SLOTS + slot] = t
        used[owner] = slot + 1
        return carry

    lax.fori_loop(0, grid_rows * SLOTS, clear, 0)
    lax.fori_loop(0, grid_rows, clear_used, 0)
    lax.fori_loop(0, tile_rows, place, 0)
    for d in range(grid_rows):
        owner = me ^ d if by_distance else d
        for s in range(SLOTS):
            t = inv[owner * SLOTS + s]
            row = jnp.maximum(t, 0)
            start = pl.multiple_of(row * tile, tile)
            for j in range(inner):
                keep = jnp.logical_and(t >= 0, am_ref[row, j] != 0)
                block = a_ref[pl.ds(start, tile), j * wide : (j + 1) * wide]
                outs[d][s * tile : (s + 1) * tile, j * wide : (j + 1) * wide] = jnp.where(
                    keep, block, jnp.zeros_like(block)
                )
    cols = bm_ref.shape[1]
    width = b_ref.shape[1] // cols
    for j in range(cols):
        block = b_ref[:, j * width : (j + 1) * width]
        b_out[:, j * width : (j + 1) * width] = jnp.where(
            bm_ref[0, j] != 0, block, jnp.zeros_like(block)
        )


def pack(a_panels, a_mask, b_panels, b_mask, owner_map, grid_rows, by_distance):
    tile = a_panels.shape[0] // a_mask.shape[0]
    slots = jax.ShapeDtypeStruct((SLOTS * tile, a_panels.shape[1]), a_panels.dtype)
    vmem = pl.BlockSpec(memory_space=pltpu.VMEM)
    outs = pl.pallas_call(
        functools.partial(pack_kernel, grid_rows, by_distance),
        out_shape=[slots] * grid_rows + [jax.ShapeDtypeStruct(b_panels.shape, b_panels.dtype)],
        in_specs=[SMEM_SPEC] * 3 + [vmem] * 2,
        out_specs=[vmem] * (grid_rows + 1),
        scratch_shapes=[
            pltpu.SMEM((grid_rows * SLOTS,), jnp.int32),
            pltpu.SMEM((grid_rows,), jnp.int32),
        ],
        name="pack",
    )(owner_map, a_mask, b_mask, a_panels, b_panels)
    return outs[:-1], outs[-1]


def dot_kernel(at_ref, own_ref, prv_ref, nxt_ref, opp_ref, far_ref, b_ref, *rest):
    out_ref, wide = rest[-2], rest[-1]
    depth = own_ref.shape[2]
    me = at_ref[at_ref.shape[0] - 1]
    far = far_ref[0]
    put = lambda panel, value: wide.__setitem__(
        (slice(None), pl.ds(pl.multiple_of(panel * depth, depth), depth)), value
    )
    put(me, own_ref[0])
    put((me + 3) % 4, jnp.where(me == 0, far, prv_ref[0]))
    put((me + 1) % 4, jnp.where(me == 3, far, nxt_ref[0]))
    put((me + 2) % 4, opp_ref[0])
    out_ref[...] = jnp.dot(
        wide[...], b_ref[...], preferred_element_type=jnp.float32
    ).astype(out_ref.dtype)


def chunk_product(at, parts, b_full, out, rows):
    blocks, height, depth = parts[0].shape
    cols = b_full.shape[1]
    spec = pl.BlockSpec((1, height, depth), lambda i, at: (i, 0, 0))
    operands = [at, *parts, b_full]
    in_specs = [spec] * 5 + [pl.BlockSpec(b_full.shape, lambda i, at: (0, 0))]
    aliases = {}
    if out is not None:
        aliases = {len(operands): 0}
        operands.append(out)
        in_specs.append(pl.BlockSpec(memory_space=pl.ANY))
    flops = 2 * blocks * height * b_full.shape[0] * cols
    return pl.pallas_call(
        dot_kernel,
        out_shape=jax.ShapeDtypeStruct((rows, cols), jnp.bfloat16),
        grid_spec=pltpu.PrefetchScalarGridSpec(
            num_scalar_prefetch=1,
            grid=(blocks,),
            in_specs=in_specs,
            out_specs=pl.BlockSpec((height, cols), lambda i, at: (at[i], 0)),
            scratch_shapes=[pltpu.VMEM((height, b_full.shape[0]), jnp.bfloat16)],
        ),
        input_output_aliases=aliases,
        cost_estimate=pl.CostEstimate(
            flops=flops, bytes_accessed=4 << 20, transcendentals=0
        ),
        name="chunk_product",
    )(*operands)


def by_row(value, distance):
    count = lax.axis_size("row")
    return lax.ppermute(value, "row", [(i, i ^ distance) for i in range(count)])


def gather_b(panel):
    mine = panel[None]
    for bit in (2, 4, 1):
        mine = jnp.concatenate([mine, by_row(mine, bit)])
    me = lax.axis_index("row")
    order = []
    for row in range(8):
        far = me ^ row
        order.append((far & 1) * 4 + (far >> 2 & 1) * 2 + (far >> 1 & 1))
    return jnp.take(mine, jnp.stack(order), axis=0, mode="clip").reshape(-1, panel.shape[1])


def along_col(own):
    me = lax.axis_index("col")
    prv = lax.ppermute(own, "col", [(0, 1), (1, 2), (2, 3)])
    nxt = lax.ppermute(own, "col", [(3, 2), (2, 1), (1, 0)])
    passed = jnp.where(me == 2, prv, jnp.where(me == 1, nxt, own))
    opp = lax.ppermute(passed, "col", [(2, 3), (1, 0), (0, 2), (3, 1)])
    far = lax.ppermute(own, "col", [(0, 3), (3, 0)])
    return [own, prv, nxt, opp, far]


def on_8_by_4(a_panels, a_mask, b_panels, b_mask, owner_map):
    packed, panel_b = pack(a_panels, a_mask, b_panels, b_mask, owner_map, 8, True)
    me = lax.axis_index("row")
    moved = [packed[0]] + [by_row(packed[d], d) for d in range(1, 8)]
    rows = 8 * packed[0].shape[0]
    chunks = [(0, 1), (2, 3, 4, 5), (6, 7)]
    gathered = [along_col(jnp.stack([moved[d] for d in chunk])) for chunk in chunks]
    b_full = gather_b(panel_b)
    out = None
    for chunk, parts in zip(chunks, gathered):
        at = jnp.stack([me ^ d for d in chunk] + [lax.axis_index("col")])
        out = chunk_product(at, parts, b_full, out, rows)
    return out


def on_any(a_panels, a_mask, b_panels, b_mask, owner_map):
    grid_rows = lax.axis_size("row")
    packed, panel_b = pack(a_panels, a_mask, b_panels, b_mask, owner_map, grid_rows, False)
    moved = lax.all_to_all(jnp.stack(packed), "row", split_axis=0, concat_axis=0, tiled=True)
    whole_a = lax.all_gather(moved, "col", axis=2, tiled=True)
    whole_b = lax.all_gather(panel_b, "row", axis=0, tiled=True)
    whole_a = whole_a.reshape(-1, whole_b.shape[0])
    return jnp.dot(whole_a, whole_b, preferred_element_type=jnp.float32).astype(jnp.bfloat16)


def solution(mesh):
    placed = (P("row", "col"), P("row", "col"), P("row", "col"), P("row", "col"), P("row", None))
    sizes = (mesh.shape["row"], mesh.shape["col"])
    return jax.shard_map(
        on_8_by_4 if sizes == (8, 4) else on_any,
        mesh=mesh,
        in_specs=placed,
        out_specs=P("row", "col"),
        check_vma=False,
    )
```

```python
import functools
import jax
import jax.numpy as jnp
from jax import lax
from jax.experimental import pallas as pl
from jax.experimental.pallas import tpu as pltpu
from jax.sharding import PartitionSpec as P

SLOTS = 2
SMEM = pl.BlockSpec(memory_space=pltpu.SMEM)
VMEM = pl.BlockSpec(memory_space=pltpu.VMEM)
HBM = pl.BlockSpec(memory_space=pltpu.HBM)
ANY = pl.BlockSpec(memory_space=pl.ANY)


def pack_kernel(owners_of, owner_hbm, am_hbm, bm_hbm, a_hbm, b_hbm, *rest):
    outs, b_out = rest[:-9], rest[-9]
    owner_ref, am_ref, bm_ref, a_ref, b_ref, inv, used, sems = rest[-8:]
    inner, tile_rows = am_ref.shape
    tile = a_ref.shape[0] // tile_rows
    wide = a_ref.shape[1] // inner
    copies = [
        pltpu.make_async_copy(source, target, sems.at[i])
        for i, (source, target) in enumerate(
            (
                (owner_hbm, owner_ref),
                (am_hbm, am_ref),
                (a_hbm, a_ref),
                (bm_hbm, bm_ref),
                (b_hbm, b_ref),
            )
        )
    ]
    for copy in copies:
        copy.start()

    def clear(i, carry):
        inv[i] = -1
        return carry

    def clear_used(i, carry):
        used[i] = 0
        return carry

    def place(t, carry):
        owner = owner_ref[0, t]
        slot = used[owner]
        inv[owner * SLOTS + slot] = t
        used[owner] = slot + 1
        return carry

    lax.fori_loop(0, inv.shape[0], clear, 0)
    lax.fori_loop(0, used.shape[0], clear_used, 0)
    copies[0].wait()
    lax.fori_loop(0, tile_rows, place, 0)
    copies[1].wait()
    copies[2].wait()
    for out, owners in zip(outs, owners_of(lax.axis_index("row"))):
        for d, owner in enumerate(owners):
            for s in range(SLOTS):
                t = inv[owner * SLOTS + s]
                row = jnp.maximum(t, 0)
                start = pl.multiple_of(row * tile, tile)
                for j in range(inner):
                    keep = jnp.logical_and(t >= 0, am_ref[j, row] != 0)
                    block = a_ref[pl.ds(start, tile), j * wide : (j + 1) * wide]
                    out[d, s * tile : (s + 1) * tile, j * wide : (j + 1) * wide] = jnp.where(
                        keep, block, jnp.zeros_like(block)
                    )
    copies[3].wait()
    copies[4].wait()
    cols = bm_ref.shape[1]
    width = b_ref.shape[1] // cols
    height = b_ref.shape[0]
    for j in range(cols):
        block = b_ref[:, j * width : (j + 1) * width]
        block = jnp.where(bm_ref[0, j] != 0, block, jnp.zeros_like(block))
        if len(b_out.shape) == 2:
            b_out[:, j * width : (j + 1) * width] = block
        else:
            piece, at = divmod(j * width, b_out.shape[2])
            piece, up = divmod(piece * height, b_out.shape[1])
            b_out[piece, up : up + height, at : at + width] = block


def pack(a_panels, a_mask, b_panels, b_mask, owner_map, owners_of, grid_rows, b_shape):
    tile = a_panels.shape[0] // a_mask.shape[0]
    groups = [len(owners) for owners in owners_of(0)]
    operands = [owner_map.T, a_mask.T, b_mask, a_panels, b_panels]
    return pl.pallas_call(
        functools.partial(pack_kernel, owners_of),
        out_shape=[
            jax.ShapeDtypeStruct((count, SLOTS * tile, a_panels.shape[1]), a_panels.dtype)
            for count in groups
        ]
        + [jax.ShapeDtypeStruct(b_shape, b_panels.dtype)],
        in_specs=[HBM] * 5,
        out_specs=[VMEM] * (len(groups) + 1),
        scratch_shapes=[pltpu.SMEM(x.shape, x.dtype) for x in operands[:3]]
        + [pltpu.VMEM(x.shape, x.dtype) for x in operands[3:]]
        + [
            pltpu.SMEM((grid_rows * SLOTS,), jnp.int32),
            pltpu.SMEM((grid_rows,), jnp.int32),
            pltpu.SemaphoreType.DMA((5,)),
        ],
        compiler_params=pltpu.CompilerParams(vmem_limit_bytes=60 << 20),
        name="pack",
    )(*operands)


def dot_kernel(first, own_ref, one_ref, two_ref, three_ref, b_ref, *rest):
    out_ref, done, sems = rest[-3:]
    blocks, height, depth = own_ref.shape
    me, col = lax.axis_index("row"), lax.axis_index("col")
    copies = []
    for i in range(blocks):
        total = None
        for far, ref in enumerate((own_ref, one_ref, two_ref, three_ref)):
            rows = pl.ds(pl.multiple_of((col ^ far) * depth, depth), depth)
            term = jnp.dot(ref[i], b_ref[rows, :], preferred_element_type=jnp.float32)
            total = term if total is None else total + term
        done[i] = total.astype(done.dtype)
        start = pl.multiple_of((me ^ (first + i)) * height, height)
        copy = pltpu.make_async_copy(
            done.at[i], out_ref.at[pl.ds(start, height), :], sems.at[i]
        )
        copy.start()
        copies.append(copy)
    for copy in copies:
        copy.wait()


def chunk_product(first, parts, b_full, out, rows):
    blocks, height, depth = parts[0].shape
    cols = b_full.shape[1]
    operands = [*parts, b_full]
    in_specs = [VMEM] * 5
    aliases = {}
    if out is not None:
        aliases = {len(operands): 0}
        operands.append(out)
        in_specs.append(ANY)
    flops = 2 * blocks * height * b_full.shape[0] * cols
    return pl.pallas_call(
        functools.partial(dot_kernel, first),
        out_shape=jax.ShapeDtypeStruct((rows, cols), jnp.bfloat16),
        in_specs=in_specs,
        out_specs=ANY,
        scratch_shapes=[
            pltpu.VMEM((blocks, height, cols), jnp.bfloat16),
            pltpu.SemaphoreType.DMA((blocks,)),
        ],
        input_output_aliases=aliases,
        compiler_params=pltpu.CompilerParams(vmem_limit_bytes=24 << 20),
        cost_estimate=pl.CostEstimate(flops=flops, bytes_accessed=4 << 20, transcendentals=0),
        name="chunk_product",
    )(*operands)


def after(value, *earlier):
    return lax.optimization_barrier((value, *earlier))[0]


def by_row(value, distance):
    return lax.ppermute(value, "row", [(i, i ^ distance) for i in range(8)])


def by_col(value, pairs):
    return lax.ppermute(value, "col", pairs)


def join_kernel(kept_ref, came_ref, b_ref, *outs):
    for chip, out in enumerate(outs, 1):
        out[0] = kept_ref[chip]
        out[1] = came_ref[chip]
        out[2:] = b_ref[...]


def join(kept, came, b_blocks):
    chunk = jax.ShapeDtypeStruct((2 + b_blocks.shape[0], *kept.shape[1:]), kept.dtype)
    return pl.pallas_call(
        join_kernel,
        out_shape=[chunk] * 3,
        in_specs=[VMEM] * 3,
        out_specs=[VMEM] * 3,
        compiler_params=pltpu.CompilerParams(vmem_limit_bytes=16 << 20),
        name="join",
    )(kept, came, b_blocks)


def order_b_kernel(mine_ref, other_ref, out_ref):
    me = lax.axis_index("row")
    height, width = mine_ref.shape[2:]
    cols = out_ref.shape[1]
    tile = mine_ref.shape[1] * height * width // cols
    for core in range(2):
        for chip in range(4):
            far = (me >> 1) ^ chip
            top = (2 * chip + core) * tile
            for ref, same in ((mine_ref, True), (other_ref, False)):

                @pl.when((me & 1 == core) == same)
                def _():
                    for j in range(cols // width):
                        piece, up = divmod(j * tile, height)
                        out_ref[top : top + tile, j * width : (j + 1) * width] = ref[
                            far, piece, up : up + tile, :
                        ]


def order_b(mine, other, shape):
    return pl.pallas_call(
        order_b_kernel,
        out_shape=jax.ShapeDtypeStruct(shape, mine.dtype),
        in_specs=[VMEM] * 2,
        out_specs=VMEM,
        compiler_params=pltpu.CompilerParams(vmem_limit_bytes=16 << 20),
        name="order_b",
    )(mine, other)


PAIRS = {
    1: [(0, 1), (1, 0), (2, 3), (3, 2)],
    2: [(2, 3), (1, 0), (0, 2), (3, 1)],
    3: [(0, 3), (3, 0), (1, 2), (2, 1)],
}


def first_hops(own):
    return by_col(own, PAIRS[3]), by_col(own, PAIRS[1])


def last_hop(own, three):
    col = lax.axis_index("col")
    return by_col(jnp.where((col == 1) | (col == 2), three, own), PAIRS[2])


def on_8_by_4(a_panels, a_mask, b_panels, b_mask, owner_map):
    def owners_of(me):
        return [me ^ (2 * chip) for chip in range(4)], [me ^ (2 * chip + 1) for chip in range(4)]

    height = SLOTS * b_panels.shape[0]
    width = a_panels.shape[1]
    b_shape = (b_panels.shape[0] * b_panels.shape[1] // (height * width), height, width)
    kept, sent, b_blocks = pack(
        a_panels, a_mask, b_panels, b_mask, owner_map, owners_of, 8, b_shape
    )
    came = by_row(sent, 1)
    near = jnp.stack([kept[0], came[0]])
    near_3, near_1 = first_hops(near)
    x, y, diagonal = join(kept, came, b_blocks)
    x, y = by_row(x, 2), by_row(y, 4)
    side = jnp.concatenate([x[:2], y[:2]])
    side_3, side_1 = first_hops(side)
    near_2 = last_hop(after(near, side), near_3)
    both = by_row(after(diagonal, side, near_3, near_1), 6)
    diagonal = both[:2]
    diagonal_3, diagonal_1 = first_hops(after(diagonal, near_1, near_2))
    mine = jnp.stack([b_blocks, x[2:], y[2:], both[2:]])
    mine = after(mine, side_3, side_1)
    b_full = order_b(mine, by_row(mine, 1), (8 * b_panels.shape[0], b_panels.shape[1]))
    side_2 = last_hop(after(side, side_1), side_3)
    rows = 8 * kept.shape[1]
    out = chunk_product(0, [near, near_1, near_2, near_3], b_full, None, rows)
    diagonal, diagonal_1, out = lax.optimization_barrier((diagonal, diagonal_1, out))
    diagonal_2 = last_hop(diagonal, diagonal_3)
    out = chunk_product(2, [side, side_1, side_2, side_3], b_full, out, rows)
    return chunk_product(
        6, [diagonal, diagonal_1, diagonal_2, diagonal_3], b_full, out, rows
    )


def on_any(a_panels, a_mask, b_panels, b_mask, owner_map):
    grid_rows = lax.axis_size("row")
    packed, panel_b = pack(
        a_panels, a_mask, b_panels, b_mask, owner_map, lambda me: [list(range(grid_rows))], grid_rows,
        b_panels.shape,
    )
    moved = lax.all_to_all(packed, "row", split_axis=0, concat_axis=0, tiled=True)
    whole_a = lax.all_gather(moved, "col", axis=2, tiled=True)
    whole_b = lax.all_gather(panel_b, "row", axis=0, tiled=True)
    whole_a = whole_a.reshape(-1, whole_b.shape[0])
    return jnp.dot(whole_a, whole_b, preferred_element_type=jnp.float32).astype(jnp.bfloat16)


def solution(mesh):
    placed = (P("row", "col"), P("row", "col"), P("row", "col"), P("row", "col"), P("row", None))
    sizes = (mesh.shape["row"], mesh.shape["col"])
    return jax.shard_map(
        on_8_by_4 if sizes == (8, 4) else on_any,
        mesh=mesh,
        in_specs=placed,
        out_specs=P("row", "col"),
        check_vma=False,
    )
```

```python
import functools
import jax
import jax.numpy as jnp
from jax import lax
from jax.experimental import pallas as pl
from jax.experimental.pallas import tpu as pltpu
from jax.sharding import PartitionSpec as P

SLOTS = 2
B = "b"
SMEM = pl.BlockSpec(memory_space=pltpu.SMEM)
VMEM = pl.BlockSpec(memory_space=pltpu.VMEM)
HBM = pl.BlockSpec(memory_space=pltpu.HBM)
ANY = pl.BlockSpec(memory_space=pl.ANY)


def pack_kernel(owners_of, owner_hbm, am_hbm, bm_hbm, a_hbm, b_hbm, *rest):
    outs = rest[:-8]
    owner_ref, am_ref, bm_ref, a_ref, b_ref, inv, used, sems = rest[-8:]
    inner, tile_rows = am_ref.shape
    tile = a_ref.shape[0] // tile_rows
    wide = a_ref.shape[1] // inner
    copies = [
        pltpu.make_async_copy(source, target, sems.at[i])
        for i, (source, target) in enumerate(
            (
                (owner_hbm, owner_ref),
                (am_hbm, am_ref),
                (a_hbm, a_ref),
                (bm_hbm, bm_ref),
                (b_hbm, b_ref),
            )
        )
    ]
    for copy in copies:
        copy.start()

    def clear(i, carry):
        inv[i] = -1
        return carry

    def clear_used(i, carry):
        used[i] = 0
        return carry

    def place(t, carry):
        owner = owner_ref[0, t]
        slot = used[owner]
        inv[owner * SLOTS + slot] = t
        used[owner] = slot + 1
        return carry

    lax.fori_loop(0, inv.shape[0], clear, 0)
    lax.fori_loop(0, used.shape[0], clear_used, 0)
    copies[0].wait()
    lax.fori_loop(0, tile_rows, place, 0)
    copies[1].wait()
    copies[2].wait()
    layout = owners_of(lax.axis_index("row"))
    for out, owners in zip(outs, layout):
        for d, owner in enumerate(owners):
            if owner is None or owner is B:
                continue
            for s in range(SLOTS):
                t = inv[owner * SLOTS + s]
                row = jnp.maximum(t, 0)
                start = pl.multiple_of(row * tile, tile)
                for j in range(inner):
                    keep = jnp.logical_and(t >= 0, am_ref[j, row] != 0)
                    block = a_ref[pl.ds(start, tile), j * wide : (j + 1) * wide]
                    out[d, s * tile : (s + 1) * tile, j * wide : (j + 1) * wide] = jnp.where(
                        keep, block, jnp.zeros_like(block)
                    )
    copies[3].wait()
    copies[4].wait()
    cols = bm_ref.shape[1]
    width = b_ref.shape[1] // cols
    height = b_ref.shape[0]
    for j in range(cols):
        block = b_ref[:, j * width : (j + 1) * width]
        block = jnp.where(bm_ref[0, j] != 0, block, jnp.zeros_like(block))
        for out, owners in zip(outs, layout):
            if B in owners:
                piece, at = divmod(j * width, out.shape[2])
                piece, up = divmod(piece * height, out.shape[1])
                out[owners.index(B) + piece, up : up + height, at : at + width] = block


def pack(a_panels, a_mask, b_panels, b_mask, owner_map, owners_of, grid_rows):
    tile = a_panels.shape[0] // a_mask.shape[0]
    height, width = SLOTS * tile, a_panels.shape[1]
    b_blocks = b_panels.size // (height * width)
    counts = [
        sum(b_blocks if owner is B else 1 for owner in owners) for owners in owners_of(0)
    ]
    operands = [owner_map.T, a_mask.T, b_mask, a_panels, b_panels]
    return pl.pallas_call(
        functools.partial(pack_kernel, owners_of),
        out_shape=[
            jax.ShapeDtypeStruct((count, height, width), a_panels.dtype) for count in counts
        ],
        in_specs=[HBM] * 5,
        out_specs=[VMEM] * len(counts),
        scratch_shapes=[pltpu.SMEM(x.shape, x.dtype) for x in operands[:3]]
        + [pltpu.VMEM(x.shape, x.dtype) for x in operands[3:]]
        + [
            pltpu.SMEM((grid_rows * SLOTS,), jnp.int32),
            pltpu.SMEM((grid_rows,), jnp.int32),
            pltpu.SemaphoreType.DMA((5,)),
        ],
        compiler_params=pltpu.CompilerParams(vmem_limit_bytes=60 << 20),
        name="pack",
    )(*operands)


def dot_kernel(first, at, own_ref, one_ref, two_ref, three_ref, b_ref, *rest):
    out_ref, done, sems = rest[-3:]
    blocks, height, depth = two_ref.shape
    me, col = lax.axis_index("row"), lax.axis_index("col")
    copies = []
    for i in range(blocks):
        total = None
        terms = (own_ref[at + i], one_ref[at + i], two_ref[i], three_ref[at + i])
        for far, block in enumerate(terms):
            rows = pl.ds(pl.multiple_of((col ^ far) * depth, depth), depth)
            term = jnp.dot(block, b_ref[rows, :], preferred_element_type=jnp.float32)
            total = term if total is None else total + term
        done[i] = total.astype(done.dtype)
        start = pl.multiple_of((me ^ (first + i)) * height, height)
        copy = pltpu.make_async_copy(
            done.at[i], out_ref.at[pl.ds(start, height), :], sems.at[i]
        )
        copy.start()
        copies.append(copy)
    for copy in copies:
        copy.wait()


def chunk_product(first, at, parts, b_full, out, rows):
    blocks, height, depth = parts[2].shape
    cols = b_full.shape[1]
    operands = [*parts, b_full]
    in_specs = [VMEM] * 5
    aliases = {}
    if out is not None:
        aliases = {len(operands): 0}
        operands.append(out)
        in_specs.append(ANY)
    flops = 2 * blocks * height * b_full.shape[0] * cols
    return pl.pallas_call(
        functools.partial(dot_kernel, first, at),
        out_shape=jax.ShapeDtypeStruct((rows, cols), jnp.bfloat16),
        in_specs=in_specs,
        out_specs=ANY,
        scratch_shapes=[
            pltpu.VMEM((blocks, height, cols), jnp.bfloat16),
            pltpu.SemaphoreType.DMA((blocks,)),
        ],
        input_output_aliases=aliases,
        compiler_params=pltpu.CompilerParams(vmem_limit_bytes=24 << 20),
        cost_estimate=pl.CostEstimate(flops=flops, bytes_accessed=4 << 20, transcendentals=0),
        name="chunk_product",
    )(*operands)


def after(value, *earlier):
    return lax.optimization_barrier((value, *earlier))[0]


def by_row(value, distance):
    return lax.ppermute(value, "row", [(i, i ^ distance) for i in range(8)])


def by_col(value, pairs):
    return lax.ppermute(value, "col", pairs)


def order_b_kernel(mine_ref, other_ref, out_ref):
    me = lax.axis_index("row")
    height, width = mine_ref.shape[2:]
    cols = out_ref.shape[1]
    tile = mine_ref.shape[1] * height * width // cols
    for core in range(2):
        for chip in range(4):
            far = (me >> 1) ^ chip
            top = (2 * chip + core) * tile
            for ref, same in ((mine_ref, True), (other_ref, False)):

                @pl.when((me & 1 == core) == same)
                def _():
                    for j in range(cols // width):
                        piece, up = divmod(j * tile, height)
                        out_ref[top : top + tile, j * width : (j + 1) * width] = ref[
                            far, piece, up : up + tile, :
                        ]


def order_b(mine, other, shape):
    return pl.pallas_call(
        order_b_kernel,
        out_shape=jax.ShapeDtypeStruct(shape, mine.dtype),
        in_specs=[VMEM] * 2,
        out_specs=VMEM,
        compiler_params=pltpu.CompilerParams(vmem_limit_bytes=16 << 20),
        name="order_b",
    )(mine, other)


PAIRS = {
    1: [(0, 1), (1, 0), (2, 3), (3, 2)],
    2: [(2, 3), (1, 0), (0, 2), (3, 1)],
    3: [(0, 3), (3, 0), (1, 2), (2, 1)],
}


def first_hops(own):
    return by_col(own, PAIRS[3]), by_col(own, PAIRS[1])


def pass_kernel(own_ref, three_ref, *outs):
    col = lax.axis_index("col")
    middle = jnp.logical_or(col == 1, col == 2)
    for ref, cond in ((three_ref, middle), (own_ref, jnp.logical_not(middle))):

        @pl.when(cond)
        def _():
            at = 0
            for out in outs:
                out[...] = ref[at : at + out.shape[0]]
                at += out.shape[0]


def pass_on(own, three, counts):
    return pl.pallas_call(
        pass_kernel,
        out_shape=[jax.ShapeDtypeStruct((n, *own.shape[1:]), own.dtype) for n in counts],
        in_specs=[VMEM] * 2,
        out_specs=[VMEM] * len(counts),
        compiler_params=pltpu.CompilerParams(vmem_limit_bytes=16 << 20),
        cost_estimate=pl.CostEstimate(flops=0, bytes_accessed=1 << 20, transcendentals=0),
        name="passed",
    )(own, three)


def fill(chunk, came, chip):
    return lax.dynamic_update_slice(chunk, came[chip : chip + 1], (1, 0, 0))


def on_8_by_4(a_panels, a_mask, b_panels, b_mask, owner_map):
    def owners_of(me):
        chips = [[me ^ (2 * chip), None] for chip in range(4)]
        sent = [me ^ (2 * chip + 1) for chip in range(4)]
        return [*chips, sent, [B]]

    near, x, y, diagonal, sent, own_b = pack(
        a_panels, a_mask, b_panels, b_mask, owner_map, owners_of, 8
    )
    came = by_row(sent, 1)
    near = fill(near, came, 0)
    near_3, near_1 = first_hops(near)
    came = after(came, near)
    far = [by_row(fill(chunk, came, i), 2 * i) for i, chunk in enumerate((x, y, diagonal), 1)]
    (passed,) = pass_on(near, near_3, [2])
    near_2 = by_col(passed, PAIRS[2])
    far = jnp.concatenate(after(far, near_1, passed))
    far_3, far_1 = first_hops(far)
    own_b = after(own_b, far)
    pair = jnp.concatenate([own_b, by_row(own_b, 2)])
    came_b = by_row(pair, 4)
    passed = pass_on(far, far_3, [2, 2, 2])
    last = [by_col(piece, PAIRS[2]) for piece in passed]
    mine = jnp.concatenate([pair, after(came_b, far_1, *passed)])
    mine = mine.reshape(4, -1, *mine.shape[1:])
    b_full = order_b(mine, by_row(mine, 1), (8 * b_panels.shape[0], b_panels.shape[1]))
    rows = 8 * near.shape[1]
    out = chunk_product(0, 0, [near, near_1, near_2, near_3], b_full, None, rows)
    for i, piece in enumerate(last):
        out = chunk_product(2 * i + 2, 2 * i, [far, far_1, piece, far_3], b_full, out, rows)
    return out


def on_any(a_panels, a_mask, b_panels, b_mask, owner_map):
    grid_rows = lax.axis_size("row")
    packed, panel_b = pack(
        a_panels,
        a_mask,
        b_panels,
        b_mask,
        owner_map,
        lambda me: [list(range(grid_rows)), [B]],
        grid_rows,
    )
    height, width = b_panels.shape[0], a_panels.shape[1]
    panel_b = panel_b.reshape(-1, height, width).transpose(1, 0, 2).reshape(b_panels.shape)
    moved = lax.all_to_all(packed, "row", split_axis=0, concat_axis=0, tiled=True)
    whole_a = lax.all_gather(moved, "col", axis=2, tiled=True)
    whole_b = lax.all_gather(panel_b, "row", axis=0, tiled=True)
    whole_a = whole_a.reshape(-1, whole_b.shape[0])
    return jnp.dot(whole_a, whole_b, preferred_element_type=jnp.float32).astype(jnp.bfloat16)


def solution(mesh):
    placed = (P("row", "col"), P("row", "col"), P("row", "col"), P("row", "col"), P("row", None))
    sizes = (mesh.shape["row"], mesh.shape["col"])
    return jax.shard_map(
        on_8_by_4 if sizes == (8, 4) else on_any,
        mesh=mesh,
        in_specs=placed,
        out_specs=P("row", "col"),
        check_vma=False,
    )
```

```python
import functools
import jax
import jax.numpy as jnp
from jax import lax
from jax.experimental import pallas as pl
from jax.experimental.pallas import tpu as pltpu
from jax.sharding import PartitionSpec as P

SLOTS = 2
LAST = [3, 2, 1]
B = "b"
SMEM = pl.BlockSpec(memory_space=pltpu.SMEM)
VMEM = pl.BlockSpec(memory_space=pltpu.VMEM)
HBM = pl.BlockSpec(memory_space=pltpu.HBM)
ANY = pl.BlockSpec(memory_space=pl.ANY)


def pack_kernel(owners_of, owner_hbm, am_hbm, bm_hbm, a_hbm, b_hbm, *rest):
    outs = rest[:-8]
    owner_ref, am_ref, bm_ref, a_ref, b_ref, inv, used, sems = rest[-8:]
    inner, tile_rows = am_ref.shape
    tile = a_ref.shape[0] // tile_rows
    wide = a_ref.shape[1] // inner
    copies = [
        pltpu.make_async_copy(source, target, sems.at[i])
        for i, (source, target) in enumerate(
            (
                (owner_hbm, owner_ref),
                (am_hbm, am_ref),
                (a_hbm, a_ref),
                (bm_hbm, bm_ref),
                (b_hbm, b_ref),
            )
        )
    ]
    for copy in copies:
        copy.start()

    def clear(i, carry):
        inv[i] = -1
        return carry

    def clear_used(i, carry):
        used[i] = 0
        return carry

    def place(t, carry):
        owner = owner_ref[0, t]
        slot = used[owner]
        inv[owner * SLOTS + slot] = t
        used[owner] = slot + 1
        return carry

    lax.fori_loop(0, inv.shape[0], clear, 0)
    lax.fori_loop(0, used.shape[0], clear_used, 0)
    copies[0].wait()
    lax.fori_loop(0, tile_rows, place, 0)
    copies[1].wait()
    copies[2].wait()
    layout = owners_of(lax.axis_index("row"))
    for out, owners in zip(outs, layout):
        for d, owner in enumerate(owners):
            if owner is None or owner is B:
                continue
            for s in range(SLOTS):
                t = inv[owner * SLOTS + s]
                row = jnp.maximum(t, 0)
                start = pl.multiple_of(row * tile, tile)
                for j in range(inner):
                    keep = jnp.logical_and(t >= 0, am_ref[j, row] != 0)
                    block = a_ref[pl.ds(start, tile), j * wide : (j + 1) * wide]
                    out[d, s * tile : (s + 1) * tile, j * wide : (j + 1) * wide] = jnp.where(
                        keep, block, jnp.zeros_like(block)
                    )
    copies[3].wait()
    copies[4].wait()
    cols = bm_ref.shape[1]
    width = b_ref.shape[1] // cols
    height = b_ref.shape[0]
    for j in range(cols):
        block = b_ref[:, j * width : (j + 1) * width]
        block = jnp.where(bm_ref[0, j] != 0, block, jnp.zeros_like(block))
        for out, owners in zip(outs, layout):
            if B in owners:
                piece, at = divmod(j * width, out.shape[2])
                piece, up = divmod(piece * height, out.shape[1])
                out[owners.index(B) + piece, up : up + height, at : at + width] = block


def pack(a_panels, a_mask, b_panels, b_mask, owner_map, owners_of, grid_rows):
    tile = a_panels.shape[0] // a_mask.shape[0]
    height, width = SLOTS * tile, a_panels.shape[1]
    b_blocks = b_panels.size // (height * width)
    counts = [
        sum(b_blocks if owner is B else 1 for owner in owners) for owners in owners_of(0)
    ]
    operands = [owner_map.T, a_mask.T, b_mask, a_panels, b_panels]
    operands = [pltpu.with_memory_space_constraint(x, pltpu.HBM) for x in operands]
    return pl.pallas_call(
        functools.partial(pack_kernel, owners_of),
        out_shape=[
            jax.ShapeDtypeStruct((count, height, width), a_panels.dtype) for count in counts
        ],
        in_specs=[HBM] * 5,
        out_specs=[VMEM] * len(counts),
        scratch_shapes=[pltpu.SMEM(x.shape, x.dtype) for x in operands[:3]]
        + [pltpu.VMEM(x.shape, x.dtype) for x in operands[3:]]
        + [
            pltpu.SMEM((grid_rows * SLOTS,), jnp.int32),
            pltpu.SMEM((grid_rows,), jnp.int32),
            pltpu.SemaphoreType.DMA((5,)),
        ],
        compiler_params=pltpu.CompilerParams(vmem_limit_bytes=16 << 20),
        name="pack",
    )(*operands)


def dot_kernel(first, at, own_ref, one_ref, two_ref, three_ref, b_ref, *rest):
    out_ref, done, sems = rest[-3:]
    blocks, height, depth = two_ref.shape
    me, col = lax.axis_index("row"), lax.axis_index("col")
    copies = []
    for i in range(blocks):
        total = None
        terms = (own_ref[at + i], one_ref[at + i], two_ref[i], three_ref[at + i])
        for far, block in enumerate(terms):
            rows = pl.ds(pl.multiple_of((col ^ far) * depth, depth), depth)
            term = jnp.dot(block, b_ref[rows, :], preferred_element_type=jnp.float32)
            total = term if total is None else total + term
        done[i] = total.astype(done.dtype)
        start = pl.multiple_of((me ^ (first + i)) * height, height)
        copy = pltpu.make_async_copy(
            done.at[i], out_ref.at[pl.ds(start, height), :], sems.at[i]
        )
        copy.start()
        copies.append(copy)
    for copy in copies:
        copy.wait()


def chunk_product(first, at, parts, b_full, out, rows):
    blocks, height, depth = parts[2].shape
    cols = b_full.shape[1]
    operands = [*parts, b_full]
    in_specs = [VMEM] * 5
    aliases = {}
    if out is not None:
        aliases = {len(operands): 0}
        operands.append(out)
        in_specs.append(ANY)
    flops = 2 * blocks * height * b_full.shape[0] * cols
    return pl.pallas_call(
        functools.partial(dot_kernel, first, at),
        out_shape=jax.ShapeDtypeStruct((rows, cols), jnp.bfloat16),
        in_specs=in_specs,
        out_specs=ANY,
        scratch_shapes=[
            pltpu.VMEM((blocks, height, cols), jnp.bfloat16),
            pltpu.SemaphoreType.DMA((blocks,)),
        ],
        input_output_aliases=aliases,
        compiler_params=pltpu.CompilerParams(vmem_limit_bytes=24 << 20),
        cost_estimate=pl.CostEstimate(flops=flops, bytes_accessed=4 << 20, transcendentals=0),
        name="chunk_product",
    )(*operands)


def after(value, *earlier):
    return lax.optimization_barrier((value, *earlier))[0]


def by_row(value, distance):
    return lax.ppermute(value, "row", [(i, i ^ distance) for i in range(8)])


def by_col(value, pairs):
    return lax.ppermute(value, "col", pairs)


def order_b_kernel(mine_ref, other_ref, out_ref):
    me = lax.axis_index("row")
    height, width = mine_ref.shape[2:]
    cols = out_ref.shape[1]
    tile = mine_ref.shape[1] * height * width // cols
    for core in range(2):
        for chip in range(4):
            far = (me >> 1) ^ chip
            top = (2 * chip + core) * tile
            for ref, same in ((mine_ref, True), (other_ref, False)):

                @pl.when((me & 1 == core) == same)
                def _():
                    for j in range(cols // width):
                        piece, up = divmod(j * tile, height)
                        out_ref[top : top + tile, j * width : (j + 1) * width] = ref[
                            far, piece, up : up + tile, :
                        ]


def order_b(mine, other, shape):
    return pl.pallas_call(
        order_b_kernel,
        out_shape=jax.ShapeDtypeStruct(shape, mine.dtype),
        in_specs=[VMEM] * 2,
        out_specs=VMEM,
        compiler_params=pltpu.CompilerParams(vmem_limit_bytes=16 << 20),
        name="order_b",
    )(mine, other)


PAIRS = {
    1: [(0, 1), (1, 0), (2, 3), (3, 2)],
    2: [(2, 3), (1, 0), (0, 2), (3, 1)],
    3: [(0, 3), (3, 0), (1, 2), (2, 1)],
}


def first_hops(own):
    return by_col(own, PAIRS[3]), by_col(own, PAIRS[1])


def pass_kernel(own_ref, three_ref, *outs):
    col = lax.axis_index("col")
    middle = jnp.logical_or(col == 1, col == 2)
    for ref, cond in ((three_ref, middle), (own_ref, jnp.logical_not(middle))):

        @pl.when(cond)
        def _():
            at = 0
            for out in outs:
                out[...] = ref[at : at + out.shape[0]]
                at += out.shape[0]


def pass_on(own, three, counts):
    return pl.pallas_call(
        pass_kernel,
        out_shape=[jax.ShapeDtypeStruct((n, *own.shape[1:]), own.dtype) for n in counts],
        in_specs=[VMEM] * 2,
        out_specs=[VMEM] * len(counts),
        compiler_params=pltpu.CompilerParams(vmem_limit_bytes=16 << 20),
        cost_estimate=pl.CostEstimate(flops=0, bytes_accessed=1 << 20, transcendentals=0),
        name="passed",
    )(own, three)


def fill(chunk, came, chip):
    return lax.dynamic_update_slice(chunk, came[chip : chip + 1], (1, 0, 0))


def on_8_by_4(a_panels, a_mask, b_panels, b_mask, owner_map):
    def owners_of(me):
        chips = [[me ^ (2 * chip), None] for chip in range(4)]
        sent = [me ^ (2 * chip + 1) for chip in range(4)]
        return [*chips, sent, [B]]

    near, x, y, diagonal, sent, own_b = pack(
        a_panels, a_mask, b_panels, b_mask, owner_map, owners_of, 8
    )
    came = by_row(sent, 1)
    near = fill(near, came, 0)
    near_3, near_1 = first_hops(near)
    came = after(came, near)
    far = [by_row(fill(chunk, came, i), 2 * i) for i, chunk in enumerate((x, y, diagonal), 1)]
    (passed,) = pass_on(near, near_3, [2])
    near_2 = by_col(passed, PAIRS[2])
    far = jnp.concatenate(after(far, near_1, near_2))
    far_3, far_1 = first_hops(far)
    own_b = after(own_b, far)
    pair = jnp.concatenate([own_b, by_row(own_b, 2)])
    came_b = by_row(pair, 4)
    passed = pass_on(far, far_3, LAST)
    last = [by_col(piece, PAIRS[2]) for piece in passed]
    mine = jnp.concatenate([pair, after(came_b, far_1, *passed)])
    mine = mine.reshape(4, -1, *mine.shape[1:])
    b_full = order_b(mine, by_row(mine, 1), (8 * b_panels.shape[0], b_panels.shape[1]))
    rows = 8 * near.shape[1]
    out = chunk_product(0, 0, [near, near_1, near_2, near_3], b_full, None, rows)
    at = 0
    for piece in last:
        out = chunk_product(2 + at, at, [far, far_1, piece, far_3], b_full, out, rows)
        at += piece.shape[0]
    return out


def on_any(a_panels, a_mask, b_panels, b_mask, owner_map):
    grid_rows = lax.axis_size("row")
    packed, panel_b = pack(
        a_panels,
        a_mask,
        b_panels,
        b_mask,
        owner_map,
        lambda me: [list(range(grid_rows)), [B]],
        grid_rows,
    )
    height, width = b_panels.shape[0], a_panels.shape[1]
    panel_b = panel_b.reshape(-1, height, width).transpose(1, 0, 2).reshape(b_panels.shape)
    moved = lax.all_to_all(packed, "row", split_axis=0, concat_axis=0, tiled=True)
    whole_a = lax.all_gather(moved, "col", axis=2, tiled=True)
    whole_b = lax.all_gather(panel_b, "row", axis=0, tiled=True)
    whole_a = whole_a.reshape(-1, whole_b.shape[0])
    return jnp.dot(whole_a, whole_b, preferred_element_type=jnp.float32).astype(jnp.bfloat16)


def solution(mesh):
    placed = (P("row", "col"), P("row", "col"), P("row", "col"), P("row", "col"), P("row", None))
    sizes = (mesh.shape["row"], mesh.shape["col"])
    return jax.shard_map(
        on_8_by_4 if sizes == (8, 4) else on_any,
        mesh=mesh,
        in_specs=placed,
        out_specs=P("row", "col"),
        check_vma=False,
    )
```

```python
import functools
import jax
import jax.numpy as jnp
from jax import lax
from jax.experimental import pallas as pl
from jax.experimental.pallas import tpu as pltpu
from jax.sharding import PartitionSpec as P

SLOTS = 2
LAST = [3, 2, 1]
B = "b"
SMEM = pl.BlockSpec(memory_space=pltpu.SMEM)
VMEM = pl.BlockSpec(memory_space=pltpu.VMEM)
HBM = pl.BlockSpec(memory_space=pltpu.HBM)
ANY = pl.BlockSpec(memory_space=pl.ANY)


def pack_kernel(owners_of, owner_hbm, am_hbm, bm_hbm, a_hbm, b_hbm, *rest):
    outs = rest[:-8]
    owner_ref, am_ref, bm_ref, a_ref, b_ref, inv, used, sems = rest[-8:]
    inner, tile_rows = am_ref.shape
    tile = a_ref.shape[0] // tile_rows
    wide = a_ref.shape[1] // inner
    copies = [
        pltpu.make_async_copy(source, target, sems.at[i])
        for i, (source, target) in enumerate(
            (
                (owner_hbm, owner_ref),
                (am_hbm, am_ref),
                (a_hbm, a_ref),
                (bm_hbm, bm_ref),
                (b_hbm, b_ref),
            )
        )
    ]
    for copy in copies:
        copy.start()

    def clear(i, carry):
        inv[i] = -1
        return carry

    def clear_used(i, carry):
        used[i] = 0
        return carry

    def place(t, carry):
        owner = owner_ref[0, t]
        slot = used[owner]
        inv[owner * SLOTS + slot] = t
        used[owner] = slot + 1
        return carry

    lax.fori_loop(0, inv.shape[0], clear, 0)
    lax.fori_loop(0, used.shape[0], clear_used, 0)
    copies[0].wait()
    lax.fori_loop(0, tile_rows, place, 0)
    copies[1].wait()
    copies[2].wait()
    layout = owners_of(lax.axis_index("row"))
    for out, owners in zip(outs, layout):
        for d, owner in enumerate(owners):
            if owner is None or owner is B:
                continue
            for s in range(SLOTS):
                t = inv[owner * SLOTS + s]
                row = jnp.maximum(t, 0)
                start = pl.multiple_of(row * tile, tile)
                for j in range(inner):
                    keep = jnp.logical_and(t >= 0, am_ref[j, row] != 0)
                    block = a_ref[pl.ds(start, tile), j * wide : (j + 1) * wide]
                    out[d, s * tile : (s + 1) * tile, j * wide : (j + 1) * wide] = jnp.where(
                        keep, block, jnp.zeros_like(block)
                    )
    copies[3].wait()
    copies[4].wait()
    cols = bm_ref.shape[1]
    width = b_ref.shape[1] // cols
    height = b_ref.shape[0]
    for j in range(cols):
        block = b_ref[:, j * width : (j + 1) * width]
        block = jnp.where(bm_ref[0, j] != 0, block, jnp.zeros_like(block))
        for out, owners in zip(outs, layout):
            if B in owners:
                piece, at = divmod(j * width, out.shape[2])
                piece, up = divmod(piece * height, out.shape[1])
                out[owners.index(B) + piece, up : up + height, at : at + width] = block


def pack(a_panels, a_mask, b_panels, b_mask, owner_map, owners_of, grid_rows):
    tile = a_panels.shape[0] // a_mask.shape[0]
    height, width = SLOTS * tile, a_panels.shape[1]
    b_blocks = b_panels.size // (height * width)
    counts = [
        sum(b_blocks if owner is B else 1 for owner in owners) for owners in owners_of(0)
    ]
    operands = [owner_map.T, a_mask.T, b_mask, a_panels, b_panels]
    operands = [pltpu.with_memory_space_constraint(x, pltpu.HBM) for x in operands]
    return pl.pallas_call(
        functools.partial(pack_kernel, owners_of),
        out_shape=[
            jax.ShapeDtypeStruct((count, height, width), a_panels.dtype) for count in counts
        ],
        in_specs=[HBM] * 5,
        out_specs=[VMEM] * len(counts),
        scratch_shapes=[pltpu.SMEM(x.shape, x.dtype) for x in operands[:3]]
        + [pltpu.VMEM(x.shape, x.dtype) for x in operands[3:]]
        + [
            pltpu.SMEM((grid_rows * SLOTS,), jnp.int32),
            pltpu.SMEM((grid_rows,), jnp.int32),
            pltpu.SemaphoreType.DMA((5,)),
        ],
        compiler_params=pltpu.CompilerParams(vmem_limit_bytes=16 << 20),
        name="pack",
    )(*operands)


def dot_kernel(first, at, own_ref, one_ref, two_ref, three_ref, b_ref, *rest):
    out_ref, done, sems = rest[-3:]
    blocks, height, depth = two_ref.shape
    me, col = lax.axis_index("row"), lax.axis_index("col")
    copies = []
    for i in range(blocks):
        total = None
        terms = (own_ref[at + i], one_ref[at + i], two_ref[i], three_ref[at + i])
        for far, block in enumerate(terms):
            rows = pl.ds(pl.multiple_of((col ^ far) * depth, depth), depth)
            term = jnp.dot(block, b_ref[rows, :], preferred_element_type=jnp.float32)
            total = term if total is None else total + term
        done[i] = total.astype(done.dtype)
        start = pl.multiple_of((me ^ (first + i)) * height, height)
        copy = pltpu.make_async_copy(
            done.at[i], out_ref.at[pl.ds(start, height), :], sems.at[i]
        )
        copy.start()
        copies.append(copy)
    for copy in copies:
        copy.wait()


def chunk_product(first, at, parts, b_full, out, rows):
    blocks, height, depth = parts[2].shape
    cols = b_full.shape[1]
    operands = [*parts, b_full]
    in_specs = [VMEM] * 5
    aliases = {}
    if out is not None:
        aliases = {len(operands): 0}
        operands.append(out)
        in_specs.append(ANY)
    flops = 2 * blocks * height * b_full.shape[0] * cols
    return pl.pallas_call(
        functools.partial(dot_kernel, first, at),
        out_shape=jax.ShapeDtypeStruct((rows, cols), jnp.bfloat16),
        in_specs=in_specs,
        out_specs=ANY,
        scratch_shapes=[
            pltpu.VMEM((blocks, height, cols), jnp.bfloat16),
            pltpu.SemaphoreType.DMA((blocks,)),
        ],
        input_output_aliases=aliases,
        compiler_params=pltpu.CompilerParams(vmem_limit_bytes=24 << 20),
        cost_estimate=pl.CostEstimate(flops=flops, bytes_accessed=4 << 20, transcendentals=0),
        name="chunk_product",
    )(*operands)


def after(value, *earlier):
    return lax.optimization_barrier((value, *earlier))[0]


def by_row(value, distance):
    return lax.ppermute(value, "row", [(i, i ^ distance) for i in range(8)])


def by_col(value, pairs):
    return lax.ppermute(value, "col", pairs)


def order_b_kernel(*refs):
    out_ref = refs[-1]
    me = lax.axis_index("row")
    blocks, height, width = refs[0].shape
    blocks = blocks // 2
    cols = out_ref.shape[1]
    tile = blocks * height * width // cols
    for far, ref in enumerate(refs[:-1]):
        for core in range(2):
            row = me ^ (2 * far + core)
            top = pl.multiple_of(row * tile, tile)
            for j in range(cols // width):
                piece, up = divmod(j * tile, height)
                out_ref[pl.ds(top, tile), j * width : (j + 1) * width] = ref[
                    core * blocks + piece, up : up + tile, :
                ]


def order_b(pairs, shape):
    return pl.pallas_call(
        order_b_kernel,
        out_shape=jax.ShapeDtypeStruct(shape, pairs[0].dtype),
        in_specs=[VMEM] * len(pairs),
        out_specs=VMEM,
        compiler_params=pltpu.CompilerParams(vmem_limit_bytes=16 << 20),
        name="order_b",
    )(*pairs)


PAIRS = {
    1: [(0, 1), (1, 0), (2, 3), (3, 2)],
    2: [(2, 3), (1, 0), (0, 2), (3, 1)],
    3: [(0, 3), (3, 0), (1, 2), (2, 1)],
}


def first_hops(own):
    return by_col(own, PAIRS[3]), by_col(own, PAIRS[1])


def pass_kernel(own_ref, three_ref, *outs):
    col = lax.axis_index("col")
    middle = jnp.logical_or(col == 1, col == 2)
    for ref, cond in ((three_ref, middle), (own_ref, jnp.logical_not(middle))):

        @pl.when(cond)
        def _():
            at = 0
            for out in outs:
                out[...] = ref[at : at + out.shape[0]]
                at += out.shape[0]


def pass_on(own, three, counts):
    return pl.pallas_call(
        pass_kernel,
        out_shape=[jax.ShapeDtypeStruct((n, *own.shape[1:]), own.dtype) for n in counts],
        in_specs=[VMEM] * 2,
        out_specs=[VMEM] * len(counts),
        compiler_params=pltpu.CompilerParams(vmem_limit_bytes=16 << 20),
        cost_estimate=pl.CostEstimate(flops=0, bytes_accessed=1 << 20, transcendentals=0),
        name="passed",
    )(own, three)


def fill(chunk, came, chip):
    return lax.dynamic_update_slice(chunk, came[chip : chip + 1], (1, 0, 0))


def on_8_by_4(a_panels, a_mask, b_panels, b_mask, owner_map):
    def owners_of(me):
        chips = [[me ^ (2 * chip), None] for chip in range(4)]
        sent = [me ^ (2 * chip + 1) for chip in range(4)]
        return [*chips, sent, [B]]

    near, x, y, diagonal, sent, own_b = pack(
        a_panels, a_mask, b_panels, b_mask, owner_map, owners_of, 8
    )
    came = by_row(sent, 1)
    near = fill(near, came, 0)
    near_3, near_1 = first_hops(near)
    came = after(came, near)
    far = [by_row(fill(chunk, came, i), 2 * i) for i, chunk in enumerate((x, y, diagonal), 1)]
    (passed,) = pass_on(near, near_3, [2])
    near_2 = by_col(passed, PAIRS[2])
    own_b = after(own_b, *far)
    far = jnp.concatenate(after(far, near_1, near_2))
    far_3, far_1 = first_hops(far)
    pair = jnp.concatenate([own_b, by_row(own_b, 1)])
    came_b = [by_row(pair, 2 * chip) for chip in range(1, 4)]
    passed = pass_on(far, far_3, LAST)
    last = [by_col(piece, PAIRS[2]) for piece in passed]
    pairs = [pair, *after(came_b, far_1, *passed)]
    b_full = order_b(pairs, (8 * b_panels.shape[0], b_panels.shape[1]))
    rows = 8 * near.shape[1]
    out = chunk_product(0, 0, [near, near_1, near_2, near_3], b_full, None, rows)
    at = 0
    for piece in last:
        out = chunk_product(2 + at, at, [far, far_1, piece, far_3], b_full, out, rows)
        at += piece.shape[0]
    return out


def on_any(a_panels, a_mask, b_panels, b_mask, owner_map):
    grid_rows = lax.axis_size("row")
    packed, panel_b = pack(
        a_panels,
        a_mask,
        b_panels,
        b_mask,
        owner_map,
        lambda me: [list(range(grid_rows)), [B]],
        grid_rows,
    )
    height, width = b_panels.shape[0], a_panels.shape[1]
    panel_b = panel_b.reshape(-1, height, width).transpose(1, 0, 2).reshape(b_panels.shape)
    moved = lax.all_to_all(packed, "row", split_axis=0, concat_axis=0, tiled=True)
    whole_a = lax.all_gather(moved, "col", axis=2, tiled=True)
    whole_b = lax.all_gather(panel_b, "row", axis=0, tiled=True)
    whole_a = whole_a.reshape(-1, whole_b.shape[0])
    return jnp.dot(whole_a, whole_b, preferred_element_type=jnp.float32).astype(jnp.bfloat16)


def solution(mesh):
    placed = (P("row", "col"), P("row", "col"), P("row", "col"), P("row", "col"), P("row", None))
    sizes = (mesh.shape["row"], mesh.shape["col"])
    return jax.shard_map(
        on_8_by_4 if sizes == (8, 4) else on_any,
        mesh=mesh,
        in_specs=placed,
        out_specs=P("row", "col"),
        check_vma=False,
    )
```

```python
import functools
import jax
import jax.numpy as jnp
from jax import lax
from jax.experimental import pallas as pl
from jax.experimental.pallas import tpu as pltpu
from jax.sharding import PartitionSpec as P

SLOTS = 2
LAST = [3, 2, 1]
B = "b"
SMEM = pl.BlockSpec(memory_space=pltpu.SMEM)
VMEM = pl.BlockSpec(memory_space=pltpu.VMEM)
HBM = pl.BlockSpec(memory_space=pltpu.HBM)
ANY = pl.BlockSpec(memory_space=pl.ANY)


def pack_kernel(owners_of, owner_hbm, am_hbm, bm_hbm, a_hbm, b_hbm, *rest):
    outs = rest[:-8]
    owner_ref, am_ref, bm_ref, a_ref, b_ref, inv, used, sems = rest[-8:]
    inner, tile_rows = am_ref.shape
    tile = a_ref.shape[0] // tile_rows
    wide = a_ref.shape[1] // inner
    copies = [
        pltpu.make_async_copy(source, target, sems.at[i])
        for i, (source, target) in enumerate(
            (
                (owner_hbm, owner_ref),
                (am_hbm, am_ref),
                (a_hbm, a_ref),
                (bm_hbm, bm_ref),
                (b_hbm, b_ref),
            )
        )
    ]
    for copy in copies:
        copy.start()

    def clear(i, carry):
        inv[i] = -1
        return carry

    def clear_used(i, carry):
        used[i] = 0
        return carry

    def place(t, carry):
        owner = owner_ref[0, t]
        slot = used[owner]
        inv[owner * SLOTS + slot] = t
        used[owner] = slot + 1
        return carry

    lax.fori_loop(0, inv.shape[0], clear, 0)
    lax.fori_loop(0, used.shape[0], clear_used, 0)
    copies[0].wait()
    lax.fori_loop(0, tile_rows, place, 0)
    copies[1].wait()
    copies[2].wait()
    layout = owners_of(lax.axis_index("row"))
    for out, owners in zip(outs, layout):
        for d, owner in enumerate(owners):
            if owner is None or owner is B:
                continue
            for s in range(SLOTS):
                t = inv[owner * SLOTS + s]
                row = jnp.maximum(t, 0)
                start = pl.multiple_of(row * tile, tile)
                for j in range(inner):
                    keep = jnp.logical_and(t >= 0, am_ref[j, row] != 0)
                    block = a_ref[pl.ds(start, tile), j * wide : (j + 1) * wide]
                    out[d, s * tile : (s + 1) * tile, j * wide : (j + 1) * wide] = jnp.where(
                        keep, block, jnp.zeros_like(block)
                    )
    copies[3].wait()
    copies[4].wait()
    cols = bm_ref.shape[1]
    width = b_ref.shape[1] // cols
    height = b_ref.shape[0]
    for j in range(cols):
        block = b_ref[:, j * width : (j + 1) * width]
        block = jnp.where(bm_ref[0, j] != 0, block, jnp.zeros_like(block))
        for out, owners in zip(outs, layout):
            if B in owners:
                piece, at = divmod(j * width, out.shape[2])
                piece, up = divmod(piece * height, out.shape[1])
                out[owners.index(B) + piece, up : up + height, at : at + width] = block


def pack(a_panels, a_mask, b_panels, b_mask, owner_map, owners_of, grid_rows):
    tile = a_panels.shape[0] // a_mask.shape[0]
    height, width = SLOTS * tile, a_panels.shape[1]
    b_blocks = b_panels.size // (height * width)
    counts = [
        sum(b_blocks if owner is B else 1 for owner in owners) for owners in owners_of(0)
    ]
    operands = [owner_map.T, a_mask.T, b_mask, a_panels, b_panels]
    operands = [pltpu.with_memory_space_constraint(x, pltpu.HBM) for x in operands]
    return pl.pallas_call(
        functools.partial(pack_kernel, owners_of),
        out_shape=[
            jax.ShapeDtypeStruct((count, height, width), a_panels.dtype) for count in counts
        ],
        in_specs=[HBM] * 5,
        out_specs=[VMEM] * len(counts),
        scratch_shapes=[pltpu.SMEM(x.shape, x.dtype) for x in operands[:3]]
        + [pltpu.VMEM(x.shape, x.dtype) for x in operands[3:]]
        + [
            pltpu.SMEM((grid_rows * SLOTS,), jnp.int32),
            pltpu.SMEM((grid_rows,), jnp.int32),
            pltpu.SemaphoreType.DMA((5,)),
        ],
        compiler_params=pltpu.CompilerParams(vmem_limit_bytes=16 << 20),
        name="pack",
    )(*operands)


def dot_kernel(first, at, own_ref, one_ref, two_ref, three_ref, b_ref, *rest):
    out_ref, done, sems = rest[-3:]
    blocks, height, depth = two_ref.shape
    me, col = lax.axis_index("row"), lax.axis_index("col")
    copies = []
    half = b_ref.shape[1] // 2
    for i in range(blocks):
        terms = (own_ref[at + i], one_ref[at + i], two_ref[i], three_ref[at + i])
        start = pl.multiple_of((me ^ (first + i)) * height, height)
        for side in range(2):
            part = slice(side * half, (side + 1) * half)
            total = None
            for far, block in enumerate(terms):
                rows = pl.ds(pl.multiple_of((col ^ far) * depth, depth), depth)
                term = jnp.dot(block, b_ref[rows, part], preferred_element_type=jnp.float32)
                total = term if total is None else total + term
            done[i, :, part] = total.astype(done.dtype)
            copy = pltpu.make_async_copy(
                done.at[i, :, part],
                out_ref.at[pl.ds(start, height), part],
                sems.at[2 * i + side],
            )
            copy.start()
            copies.append(copy)
    for copy in copies:
        copy.wait()


def chunk_product(first, at, parts, b_full, out, rows):
    blocks, height, depth = parts[2].shape
    cols = b_full.shape[1]
    operands = [*parts, b_full]
    in_specs = [VMEM] * 5
    aliases = {}
    if out is not None:
        aliases = {len(operands): 0}
        operands.append(out)
        in_specs.append(ANY)
    flops = 2 * blocks * height * b_full.shape[0] * cols
    return pl.pallas_call(
        functools.partial(dot_kernel, first, at),
        out_shape=jax.ShapeDtypeStruct((rows, cols), jnp.bfloat16),
        in_specs=in_specs,
        out_specs=ANY,
        scratch_shapes=[
            pltpu.VMEM((blocks, height, cols), jnp.bfloat16),
            pltpu.SemaphoreType.DMA((2 * blocks,)),
        ],
        input_output_aliases=aliases,
        compiler_params=pltpu.CompilerParams(vmem_limit_bytes=24 << 20),
        cost_estimate=pl.CostEstimate(flops=flops, bytes_accessed=4 << 20, transcendentals=0),
        name="chunk_product",
    )(*operands)


def after(value, *earlier):
    return lax.optimization_barrier((value, *earlier))[0]


def by_row(value, distance):
    return lax.ppermute(value, "row", [(i, i ^ distance) for i in range(8)])


def by_col(value, pairs):
    return lax.ppermute(value, "col", pairs)


def order_b_kernel(*refs):
    out_ref = refs[-1]
    me = lax.axis_index("row")
    blocks, height, width = refs[0].shape
    blocks = blocks // 2
    cols = out_ref.shape[1]
    tile = blocks * height * width // cols
    for far, ref in enumerate(refs[:-1]):
        for core in range(2):
            row = me ^ (2 * far + core)
            top = pl.multiple_of(row * tile, tile)
            for j in range(cols // width):
                piece, up = divmod(j * tile, height)
                out_ref[pl.ds(top, tile), j * width : (j + 1) * width] = ref[
                    core * blocks + piece, up : up + tile, :
                ]


def order_b(pairs, shape):
    return pl.pallas_call(
        order_b_kernel,
        out_shape=jax.ShapeDtypeStruct(shape, pairs[0].dtype),
        in_specs=[VMEM] * len(pairs),
        out_specs=VMEM,
        compiler_params=pltpu.CompilerParams(vmem_limit_bytes=16 << 20),
        name="order_b",
    )(*pairs)


PAIRS = {
    1: [(0, 1), (1, 0), (2, 3), (3, 2)],
    2: [(2, 3), (1, 0), (0, 2), (3, 1)],
    3: [(0, 3), (3, 0), (1, 2), (2, 1)],
}


def first_hops(own):
    return by_col(own, PAIRS[3]), by_col(own, PAIRS[1])


def pass_kernel(own_ref, three_ref, *outs):
    col = lax.axis_index("col")
    middle = jnp.logical_or(col == 1, col == 2)
    for ref, cond in ((three_ref, middle), (own_ref, jnp.logical_not(middle))):

        @pl.when(cond)
        def _():
            at = 0
            for out in outs:
                out[...] = ref[at : at + out.shape[0]]
                at += out.shape[0]


def pass_on(own, three, counts):
    return pl.pallas_call(
        pass_kernel,
        out_shape=[jax.ShapeDtypeStruct((n, *own.shape[1:]), own.dtype) for n in counts],
        in_specs=[VMEM] * 2,
        out_specs=[VMEM] * len(counts),
        compiler_params=pltpu.CompilerParams(vmem_limit_bytes=16 << 20),
        cost_estimate=pl.CostEstimate(flops=0, bytes_accessed=1 << 20, transcendentals=0),
        name="passed",
    )(own, three)


def fill(chunk, came, chip):
    return lax.dynamic_update_slice(chunk, came[chip : chip + 1], (1, 0, 0))


def on_8_by_4(a_panels, a_mask, b_panels, b_mask, owner_map):
    def owners_of(me):
        chips = [[me ^ (2 * chip), None] for chip in range(4)]
        sent = [me ^ (2 * chip + 1) for chip in range(4)]
        return [*chips, sent, [B]]

    near, x, y, diagonal, sent, own_b = pack(
        a_panels, a_mask, b_panels, b_mask, owner_map, owners_of, 8
    )
    came = by_row(sent, 1)
    near = fill(near, came, 0)
    near_3, near_1 = first_hops(near)
    came = after(came, near)
    far = [by_row(fill(chunk, came, i), 2 * i) for i, chunk in enumerate((x, y, diagonal), 1)]
    (passed,) = pass_on(near, near_3, [2])
    near_2 = by_col(passed, PAIRS[2])
    own_b = after(own_b, *far)
    far = jnp.concatenate(after(far, near_1, near_2))
    far_3, far_1 = first_hops(far)
    pair = jnp.concatenate([own_b, by_row(own_b, 1)])
    came_b = [by_row(pair, 2 * chip) for chip in range(1, 4)]
    passed = pass_on(far, far_3, LAST)
    last = [by_col(piece, PAIRS[2]) for piece in passed]
    pairs = [pair, *after(came_b, far_1, *passed)]
    b_full = order_b(pairs, (8 * b_panels.shape[0], b_panels.shape[1]))
    rows = 8 * near.shape[1]
    out = chunk_product(0, 0, [near, near_1, near_2, near_3], b_full, None, rows)
    at = 0
    for piece in last:
        out = chunk_product(2 + at, at, [far, far_1, piece, far_3], b_full, out, rows)
        at += piece.shape[0]
    return out


def on_any(a_panels, a_mask, b_panels, b_mask, owner_map):
    grid_rows = lax.axis_size("row")
    packed, panel_b = pack(
        a_panels,
        a_mask,
        b_panels,
        b_mask,
        owner_map,
        lambda me: [list(range(grid_rows)), [B]],
        grid_rows,
    )
    height, width = b_panels.shape[0], a_panels.shape[1]
    panel_b = panel_b.reshape(-1, height, width).transpose(1, 0, 2).reshape(b_panels.shape)
    moved = lax.all_to_all(packed, "row", split_axis=0, concat_axis=0, tiled=True)
    whole_a = lax.all_gather(moved, "col", axis=2, tiled=True)
    whole_b = lax.all_gather(panel_b, "row", axis=0, tiled=True)
    whole_a = whole_a.reshape(-1, whole_b.shape[0])
    return jnp.dot(whole_a, whole_b, preferred_element_type=jnp.float32).astype(jnp.bfloat16)


def solution(mesh):
    placed = (P("row", "col"), P("row", "col"), P("row", "col"), P("row", "col"), P("row", None))
    sizes = (mesh.shape["row"], mesh.shape["col"])
    return jax.shard_map(
        on_8_by_4 if sizes == (8, 4) else on_any,
        mesh=mesh,
        in_specs=placed,
        out_specs=P("row", "col"),
        check_vma=False,
    )
```
